512 devices in a mesh: lat: 16 (over z), lon: 32 (over x, y, core).
Axes of the slice: x: 4, y: 4, z: 16, core: 2. Of those that a mesh axis runs over, the one named last changes fastest.
Arguments:
- diffusivity: float32 [10, 512, 4096], P(None, 'lat', 'lon'), may hold values from 0.03 to 0.24
- land_mask: int32 [512, 4096], P('lat', 'lon'), may hold values 0 or 1
- obs_weights: bfloat16 [2, 8, 512, 4096], P(None, None, 'lat', 'lon'), may hold values from -0.09375 to 0.09375
- innovation: float32 [2, 16, 32, 8], P(None, 'lat', 'lon'), may hold values from -192 to 192
- precision_weights: float32 [2, 16, 32, 8], P(None, 'lat', 'lon'), may hold values from 0.5 to 4
- obs_count: int32 [16, 32], P('lat', 'lon'), may hold values from 2 to 8, as said below
Outputs:
- control: float32 [10, 512, 4096], P(None, 'lat', 'lon')
- increment: float32 [10, 512, 4096], P(None, 'lat', 'lon')
The draws below stay inside these ranges and needn't reach their ends.
Inputs may be any that keep to these rules, and one draw needn't show every extreme that they name: Tile (a, b) has valid observations in slots 0 to obs_count[a, b] - 1; some tile has 8.
All inputs are finite; a program needn't handle non-finite values. No bound on the sum of `land_mask` on one device may be relied on, other than what follows from the above.
Results may differ from the reference program's by a relative error of at most 0.0049.
Values sent between devices are 32-bit elements; how exact they have to be, the bound alone decides.
No kernel may reach another device: no remote copies, remote signals or barrier semaphores. Data moves between devices by JAX's collectives and lax.ppermute only.
A program may use at most 64 MiB of HBM per device.

```python
import math
import jax
import jax.numpy as jnp
from jax import lax

NCAT = 5
FIELDS = 10
CX = 32
CY = 128
OBS = 8
STEPS = 6
ITERS = 2
TILES_LAT = 16
TILES_LON = 32
NX = 512
NY = 4096


def draw_obs_count(key, part):
    first, second = jax.random.split(key)
    counts = jax.random.randint(first, (TILES_LAT, TILES_LON), OBS // 4, OBS + 1)
    chosen = jax.random.randint(second, (), 0, TILES_LAT * TILES_LON)
    places = lax.broadcasted_iota(jnp.int32, (TILES_LAT, TILES_LON), 0) * TILES_LON + lax.broadcasted_iota(jnp.int32, (TILES_LAT, TILES_LON), 1)
    return jnp.where(places == chosen, OBS, counts).astype(jnp.int32)


def touch_ends(result, key, low, high):
    shape = result.shape
    index_at = [jax.random.randint(jax.random.fold_in(key, axis), (), 0, shape[axis]) for axis in range(len(shape))]
    result = result.at[tuple(index_at)].set(low)
    longest = shape.index(max(shape))
    index_at[longest] = (index_at[longest] + 1) % shape[longest]
    return result.at[tuple(index_at)].set(high)


def levels(own_key, extent, cuts, least, high):
    def one(axis_at, parts):
        steps = jax.random.uniform(jax.random.fold_in(jax.random.fold_in(own_key, 6), axis_at), (parts,), jnp.float32, least / len(cuts), high / len(cuts))
        return jnp.repeat(jnp.exp(steps), extent[axis_at] // parts).reshape((-1,) + (1,) * (len(extent) - axis_at - 1))

    factor_of = one(*cuts[0])
    for cut in cuts[1:]:
        factor_of = factor_of * one(*cut)
    return factor_of


def normal_values(own_key, dims, deviation, limit, shards=(), kind=jnp.bfloat16):
    values = jax.random.normal(own_key, dims, jnp.float32) * deviation
    if len(shards) > 0:
        values = levels(own_key, dims, shards, -0.22, 0.18) * values
    return jnp.clip(values, min=-limit, max=limit).astype(kind)


def setup_inputs(seed: int = 0) -> dict:
    seeds = jax.random.split(jax.random.key(seed), 7)
    diffusivity = jnp.clip(jnp.exp(math.log(0.24) - 2.0794415 * jax.random.uniform(seeds[0], (FIELDS, NX, NY), jnp.float32) ** levels(seeds[0], (FIELDS, NX, NY), ((1, 16), (2, 32)), -0.2, 0.2)), 0.03, 0.24)
    land_mask = touch_ends((jax.random.randint(seeds[1], (NX, NY), 0, 5) < 4).astype(jnp.int32), jax.random.fold_in(seeds[1], 1), 0, 1)
    obs_weights = normal_values(seeds[2], (2, OBS, NX, NY), (CX * CY) ** -0.5, 0.09375, ((2, 16), (3, 32)))
    innovation = normal_values(seeds[3], (2, TILES_LAT, TILES_LON, OBS), 32.0, 192.0, ((1, 16), (2, 32)), jnp.float32)
    precision_weights = jnp.clip(jnp.exp(math.log(4.0) - 2.0794415 * jax.random.uniform(seeds[4], (2, TILES_LAT, TILES_LON, OBS), jnp.float32) ** levels(seeds[4], (2, TILES_LAT, TILES_LON, OBS), ((1, 16), (2, 32)), -0.2, 0.2)), 0.5, 4.0)
    obs_count = draw_obs_count(jax.random.fold_in(seeds[6], 71), 0)
    return {"diffusivity": diffusivity, "land_mask": land_mask, "obs_weights": obs_weights, "innovation": innovation, "precision_weights": precision_weights, "obs_count": obs_count}


def pad_grid(field, width):
    field = jnp.pad(field, ((0, 0), (width, width), (0, 0)))
    return jnp.concatenate([field[:, :, -width:], field, field[:, :, :width]], axis=2)


def advance(padded, east_face, north_face):
    center = padded[:, 1:-1, 1:-1]
    change = east_face[:, 1:-1, 1:] * (padded[:, 1:-1, 2:] - center)
    change = change + east_face[:, 1:-1, :-1] * (padded[:, 1:-1, :-2] - center)
    change = change + north_face[:, 1:, 1:-1] * (padded[:, 2:, 1:-1] - center)
    change = change + north_face[:, :-1, 1:-1] * (padded[:, :-2, 1:-1] - center)
    return center + change


def reference(diffusivity, land_mask, obs_weights, innovation, precision_weights, obs_count):
    ocean = land_mask.astype(jnp.float32)[None]
    scaled = pad_grid(diffusivity * ocean, 1)
    wet = pad_grid(ocean, 1)
    east = 0.5 * (scaled[:, :, :-1] * wet[:, :, 1:] + scaled[:, :, 1:] * wet[:, :, :-1])
    north = 0.5 * (scaled[:, :-1, :] * wet[:, 1:, :] + scaled[:, 1:, :] * wet[:, :-1, :])

    def diffuse(field):
        for _ in range(STEPS):
            field = advance(pad_grid(field, 1), east, north)
        return field

    def cover(field):
        return ocean * diffuse(field)

    def cover_adjoint(field):
        return diffuse(ocean * field)

    slots = lax.broadcasted_iota(jnp.int32, innovation.shape, 3)
    keep = jnp.where(slots < obs_count[None, :, :, None], precision_weights, 0.0)

    def observe(field):
        total = field.reshape(2, NCAT, NX, NY).sum(axis=1).astype(jnp.bfloat16)

        def one_row(index):
            block = lax.dynamic_slice_in_dim(obs_weights, index * CX, CX, 2).astype(jnp.float32)
            piece = lax.dynamic_slice_in_dim(total, index * CX, CX, 1).astype(jnp.float32)
            block = block.reshape(2, OBS, CX, TILES_LON, CY)
            piece = piece.reshape(2, CX, TILES_LON, CY)
            return jnp.einsum("foxby,fxby->fbo", block, piece, precision=lax.Precision.HIGHEST)

        rows = lax.map(one_row, jnp.arange(TILES_LAT, dtype=jnp.int32))
        return jnp.transpose(rows, (1, 0, 2, 3))

    def spread(weighted):
        rounded = weighted.astype(jnp.bfloat16)

        def one_row(index):
            block = lax.dynamic_slice_in_dim(obs_weights, index * CX, CX, 2).astype(jnp.float32)
            block = block.reshape(2, OBS, CX, TILES_LON, CY)
            piece = lax.dynamic_index_in_dim(rounded, index, 1, keepdims=False).astype(jnp.float32)
            back = jnp.einsum("foxby,fbo->fxby", block, piece, precision=lax.Precision.HIGHEST)
            return back.reshape(2, CX, NY)

        rows = lax.map(one_row, jnp.arange(TILES_LAT, dtype=jnp.int32))
        back = jnp.transpose(rows, (1, 0, 2, 3)).reshape(2, NX, NY)
        return jnp.repeat(back, NCAT, axis=0)

    def hessian(direction):
        return direction + cover_adjoint(spread(keep * observe(cover(direction))))

    right = cover_adjoint(spread(keep * innovation))
    control = jnp.zeros_like(right)
    residual = right
    direction = right
    norm_now = jnp.sum(residual * residual)
    for number in range(ITERS):
        image = hessian(direction)
        alpha = norm_now / jnp.sum(direction * image)
        control = control + alpha * direction
        residual = residual - alpha * image
        if number + 1 < ITERS:
            norm_next = jnp.sum(residual * residual)
            direction = residual + (norm_next / norm_now) * direction
            norm_now = norm_next
    return control, cover(control)
```

```python
import jax
import jax.numpy as jnp
from jax import lax
from jax.experimental import pallas as pl
from jax.experimental.pallas import tpu as pltpu
from jax.sharding import PartitionSpec as P

NCAT = 5
FIELDS = 10
OBS = 8
STEPS = 6
HALO = 12
EDGE = 16
ROWS = 32
COLS = 128
TALL = ROWS + 2 * EDGE
WIDE = 2 * COLS

VMEM = pl.BlockSpec(memory_space=pltpu.VMEM)
SMEM = pl.BlockSpec(memory_space=pltpu.SMEM)
PARAMS = pltpu.CompilerParams(vmem_limit_bytes=48 << 20)


def f32(*shape):
    return jax.ShapeDtypeStruct(shape, jnp.float32)


def lanes(rows):
    return lax.broadcasted_iota(jnp.int32, (rows, COLS), 1)


def rounded(values):
    return values.astype(jnp.bfloat16).astype(jnp.float32)


def pack(planes, start):
    lane = lanes(planes[0].shape[0])
    packed = jnp.zeros_like(planes[0])
    for place, plane in enumerate(planes):
        moved = pltpu.roll(plane, (HALO * place - start) % COLS, 1)
        packed = jnp.where(
            (lane >= HALO * place) & (lane < HALO * (place + 1)), moved, packed
        )
    return packed


def spread(weights, vector, f):
    total = weights[f * OBS].astype(jnp.float32) * vector[f * OBS : f * OBS + 1]
    for slot in range(1, OBS):
        at = f * OBS + slot
        total = total + weights[at].astype(jnp.float32) * vector[at : at + 1]
    return total


def observe(weights, totals):
    rows = []
    for f in range(2):
        for slot in range(OBS):
            product = weights[f * OBS + slot].astype(jnp.float32) * totals[f]
            rows.append(jnp.sum(product, axis=0, keepdims=True))
    seen = jnp.sum(jnp.concatenate(rows, axis=0), axis=1, keepdims=True)
    return jnp.broadcast_to(seen, (2 * OBS, COLS))


def strips(planes, odd, out_a, out_b, at):
    left = pack(planes, 0)
    right = pack(planes, COLS - HALO)
    rows = left.shape[0]
    out_a[at : at + rows] = jnp.where(odd, right, left)
    out_b[at : at + rows] = jnp.where(odd, left, right)


def first_kernel(
    odd_ref, count_ref, innovation_ref, precision_ref, diffusivity, mask, weights,
    base, send_a, send_b, start_vector, keep,
):
    ocean = mask[...].astype(jnp.float32)
    odd = odd_ref[0] == 1
    count = count_ref[0, 0]
    for f in range(2):
        for slot in range(OBS):
            at = f * OBS + slot
            kept = jnp.where(slot < count, precision_ref[f, slot], 0.0)
            keep[at : at + 1] = jnp.full((1, COLS), kept, jnp.float32)
            start_vector[at : at + 1] = jnp.full(
                (1, COLS), kept * innovation_ref[f, slot], jnp.float32
            )
    vector = rounded(start_vector[...])
    start_vector[...] = vector
    for k in range(FIELDS):
        base[k] = diffusivity[k] * ocean
    for f in range(2):
        base[FIELDS + f] = ocean * spread(weights, vector, f)
    strips([base[k] for k in range(FIELDS)], odd, send_a, send_b, 0)
    strips([base[FIELDS], base[FIELDS + 1]], odd, send_a, send_b, ROWS)


def widen(main, left, right, place):
    rows = main.shape[0]
    lane = lanes(rows)
    right = pltpu.roll(right, (-HALO * place) % COLS, 1)
    left = pltpu.roll(left, (COLS - HALO - HALO * place) % COLS, 1)
    side = jnp.where(lane < HALO, right, jnp.where(lane >= COLS - HALO, left, 0.0))
    return jnp.concatenate([main, side], axis=1)


def around(field, rows_by, cols_by):
    if rows_by:
        field = pltpu.roll(field, rows_by % field.shape[0], 0)
    if cols_by:
        field = pltpu.roll(field, cols_by % field.shape[1], 1)
    return field


def two_factors(scaled, ocean, ocean_east, ocean_north, field):
    east = 0.5 * (scaled * ocean_east + around(scaled, 0, -1) * ocean)
    north = 0.5 * (scaled * ocean_north + around(scaled, -1, 0) * ocean)
    west = around(east, 0, 1)
    south = around(north, 1, 0)
    middle = 1.0 - east - west - north - south
    faces = [middle, east, west, north, south]

    def step(x, faces):
        middle, east, west, north, south = faces
        return (
            middle * x
            + (east * around(x, 0, -1) + west * around(x, 0, 1))
            + (north * around(x, -1, 0) + south * around(x, 1, 0))
        )

    x = field
    for _ in range(4):
        x = step(x, faces)
    cut = EDGE - 8
    x = x[cut:-cut]
    faces = [face[cut:-cut] for face in faces]
    for _ in range(4, STEPS):
        x = step(x, faces)
    first = x[8:-8, :COLS]
    x = x * ocean[cut:-cut]
    for _ in range(STEPS):
        x = step(x, faces)
    return first, x[8:-8, :COLS] * ocean[EDGE:-EDGE, :COLS]


def sweep(scaled, oceans, fields, weights, out_x, out_y, totals):
    totals[...] = jnp.zeros_like(totals)

    def one(category, carry):
        for f in range(2):
            k = f * NCAT + category
            first, second = two_factors(
                scaled[k], oceans[0], oceans[1], oceans[2], fields[f]
            )
            out_x[k] = first
            out_y[k] = second
            totals[f] = totals[f] + second
        return carry

    lax.fori_loop(0, NCAT, one, 0)
    return observe(weights, totals)


def sided(odd, a, b):
    return jnp.where(odd, b, a), jnp.where(odd, a, b)


def second_kernel(
    odd_ref, base, got_a, got_b, above, below, weights, start_vector, keep,
    out_x, out_y, scaled, oceans, spread_out, send_a, send_b, vectors,
    fields, totals,
):
    odd = odd_ref[0] == 1
    planes = FIELDS + 2
    halves = []
    for half in range(2):
        pair = []
        for side, got in enumerate((got_a, got_b)):
            at = planes * EDGE + (2 * side + half) * EDGE
            pair.append(
                jnp.concatenate(
                    [above[at : at + EDGE], got[half * ROWS : (half + 1) * ROWS], below[at : at + EDGE]],
                    axis=0,
                )
            )
        halves.append(sided(odd, *pair))

    def whole(k, left, right, place):
        at = k * EDGE
        main = jnp.concatenate([above[at : at + EDGE], base[k], below[at : at + EDGE]], axis=0)
        return widen(main, left, right, place)

    for k in range(FIELDS):
        scaled[k] = whole(k, *halves[0], k)
    for f in range(2):
        fields[f] = whole(FIELDS + f, *halves[1], f)
    ocean = jnp.where(scaled[0] > 0.0, 1.0, 0.0)
    oceans[0] = ocean
    oceans[1] = around(ocean, 0, -1)
    oceans[2] = around(ocean, -1, 0)
    seen = sweep(scaled, oceans, fields, weights, out_x, out_y, totals)
    vector = rounded(keep[...] * seen)
    vectors[0] = seen
    vectors[1] = vector
    own = oceans[0, EDGE:-EDGE, :COLS]
    for f in range(2):
        spread_out[f] = own * spread(weights, vector, f)
    strips([spread_out[0], spread_out[1]], odd, send_a, send_b, 0)


def third_kernel(
    odd_ref, spread_in, got_a, got_b, above, below, weights, start_vector, keep,
    scaled, oceans, vectors,
    out_x, out_y, sums,
    fields, totals,
):
    odd = odd_ref[0] == 1
    pair = []
    for side, got in enumerate((got_a, got_b)):
        at = (2 + side) * EDGE
        pair.append(jnp.concatenate([above[at : at + EDGE], got[...], below[at : at + EDGE]], axis=0))
    left, right = sided(odd, *pair)
    for f in range(2):
        at = f * EDGE
        main = jnp.concatenate([above[at : at + EDGE], spread_in[f], below[at : at + EDGE]], axis=0)
        fields[f] = widen(main, left, right, f)
    later = sweep(scaled, oceans, fields, weights, out_x, out_y, totals)
    seen = vectors[0]
    vector = vectors[1]
    start = start_vector[...]
    kept = keep[...]
    terms = [
        start * seen, vector * seen, vector * later,
        seen * kept * seen, seen * kept * later, later * kept * later,
    ]
    lane = lanes(1)
    row = jnp.zeros((1, COLS), jnp.float32)
    for place, term in enumerate(terms):
        row = jnp.where(lane == place, jnp.sum(term, axis=0, keepdims=True), row)
    sums[...] = jnp.broadcast_to(row, sums.shape)


def last_kernel(sums, x_first, y_first, x_second, y_second, control, increment):
    row = jnp.sum(sums[...], axis=0, keepdims=True)
    lane = lanes(1)
    a, b, c, k00, k01, k11 = [
        jnp.sum(jnp.where(lane == place, row, 0.0), axis=1, keepdims=True) for place in range(6)
    ]
    b, c, k00, k01, k11 = [value / a for value in (b, c, k00, k01, k11)]
    alpha = 1.0 / (1.0 + b)
    beta = (c - b * b) * alpha * alpha
    share = 1.0 - alpha + beta
    below = (share * share * (1.0 + k00)) - 2.0 * share * alpha * (b + k01) + alpha * alpha * (c + k11)
    later = beta / below
    first = jnp.broadcast_to(alpha + later * share, (ROWS, COLS))
    second = jnp.broadcast_to(-later * alpha, (ROWS, COLS))
    for k in range(FIELDS):
        control[k] = first * x_first[k] + second * x_second[k]
        increment[k] = first * y_first[k] + second * y_second[k]


def per_device(diffusivity, land_mask, obs_weights, innovation, precision_weights, obs_count):
    lat_count = lax.axis_size("lat")
    lon_count = lax.axis_size("lon")
    odd = (lax.axis_index("lon") % 2).astype(jnp.int32).reshape(1)
    down = [(i, i + 1) for i in range(lat_count - 1)]
    up = [(i + 1, i) for i in range(lat_count - 1)]
    within = [(i, i ^ 1) for i in range(lon_count)]
    between = [(i, (i + 1 if i % 2 else i - 1) % lon_count) for i in range(lon_count)]
    weights = obs_weights.reshape(2 * OBS, ROWS, COLS)

    base, send_a, send_b, start_vector, keep = pl.pallas_call(
        first_kernel,
        out_shape=(f32(FIELDS + 2, ROWS, COLS), f32(2 * ROWS, COLS), f32(2 * ROWS, COLS),
                   f32(2 * OBS, COLS), f32(2 * OBS, COLS)),
        in_specs=[SMEM] * 4 + [VMEM] * 3,
        out_specs=[VMEM] * 5,
        compiler_params=PARAMS,
        name="first",
    )(odd, obs_count, innovation.reshape(2, OBS), precision_weights.reshape(2, OBS),
      diffusivity, land_mask, weights)

    def exchange(planes, send_a, send_b):
        got_a = lax.ppermute(send_a, "lon", between)
        got_b = lax.ppermute(send_b, "lon", within)
        halves = send_a.shape[0] // ROWS

        def edge(at):
            parts = [planes[:, at : at + EDGE].reshape(-1, COLS)]
            for got in (got_a, got_b):
                for half in range(halves):
                    parts.append(got[half * ROWS + at : half * ROWS + at + EDGE])
            return jnp.concatenate(parts, axis=0)

        above = lax.ppermute(edge(ROWS - EDGE), "lat", down)
        below = lax.ppermute(edge(0), "lat", up)
        return got_a, got_b, above, below

    x_first, y_first, scaled, oceans, spread_first, send_a, send_b, vectors = pl.pallas_call(
        second_kernel,
        out_shape=(f32(FIELDS, ROWS, COLS), f32(FIELDS, ROWS, COLS), f32(FIELDS, TALL, WIDE),
                   f32(3, TALL, WIDE), f32(2, ROWS, COLS), f32(ROWS, COLS), f32(ROWS, COLS),
                   f32(2, 2 * OBS, COLS)),
        in_specs=[SMEM] + [VMEM] * 8,
        out_specs=[VMEM] * 8,
        scratch_shapes=[pltpu.VMEM((2, TALL, WIDE), jnp.float32),
                        pltpu.VMEM((2, ROWS, COLS), jnp.float32)],
        compiler_params=PARAMS,
        name="second",
    )(odd, base, *exchange(base, send_a, send_b), weights, start_vector, keep)

    x_second, y_second, sums = pl.pallas_call(
        third_kernel,
        out_shape=(f32(FIELDS, ROWS, COLS), f32(FIELDS, ROWS, COLS), f32(lon_count, COLS)),
        in_specs=[SMEM] + [VMEM] * 11,
        out_specs=[VMEM] * 3,
        scratch_shapes=[pltpu.VMEM((2, TALL, WIDE), jnp.float32),
                        pltpu.VMEM((2, ROWS, COLS), jnp.float32)],
        compiler_params=PARAMS,
        name="third",
    )(odd, spread_first, *exchange(spread_first, send_a, send_b), weights, start_vector, keep,
      scaled, oceans, vectors)

    sums = lax.all_to_all(sums, "lon", 0, 0, tiled=True)
    sums = jnp.broadcast_to(jnp.sum(sums, axis=0, keepdims=True), (lat_count, COLS))
    sums = lax.all_to_all(sums, "lat", 0, 0, tiled=True)
    return pl.pallas_call(
        last_kernel,
        out_shape=(f32(FIELDS, ROWS, COLS), f32(FIELDS, ROWS, COLS)),
        in_specs=[VMEM] * 5,
        out_specs=[VMEM] * 2,
        compiler_params=PARAMS,
        name="last",
    )(sums, x_first, y_first, x_second, y_second)


def solution(mesh):
    return jax.shard_map(
        per_device,
        mesh=mesh,
        in_specs=(
            P(None, "lat", "lon"),
            P("lat", "lon"),
            P(None, None, "lat", "lon"),
            P(None, "lat", "lon", None),
            P(None, "lat", "lon", None),
            P("lat", "lon"),
        ),
        out_specs=(P(None, "lat", "lon"), P(None, "lat", "lon")),
        check_vma=False,
    )
```

```python
import jax
import jax.numpy as jnp
from jax import lax
from jax.experimental import pallas as pl
from jax.experimental.pallas import tpu as pltpu
from jax.sharding import PartitionSpec as P

NCAT = 5
FIELDS = 10
OBS = 8
STEPS = 6
HALO = 12
EDGE = 16
ROWS = 32
COLS = 128
TALL = ROWS + 2 * EDGE
TILES = 7
DEEP = 8 * TILES
GROUP = NCAT + 1
ALL = 2 * GROUP
SLOT = 2 * HALO
PACKS = 3

VMEM = pl.BlockSpec(memory_space=pltpu.VMEM)
ANY = pl.BlockSpec(memory_space=pl.ANY)
PARAMS = pltpu.CompilerParams(vmem_limit_bytes=40 << 20)


def f32(*shape):
    return jax.ShapeDtypeStruct(shape, jnp.float32)


def lanes(rows):
    return lax.broadcasted_iota(jnp.int32, (rows, COLS), 1)


def rounded(values):
    return values.astype(jnp.bfloat16).astype(jnp.float32)


def turn(plane, amount):
    amount = amount % COLS
    return plane if amount == 0 else pltpu.roll(plane, amount, 1)


def spread(weights, vector, f):
    total = weights[f * OBS].astype(jnp.float32) * vector[f * OBS : f * OBS + 1]
    for slot in range(1, OBS):
        at = f * OBS + slot
        total = total + weights[at].astype(jnp.float32) * vector[at : at + 1]
    return total


def observe(weights, totals):
    rows = []
    for f in range(2):
        for slot in range(OBS):
            product = weights[f * OBS + slot].astype(jnp.float32) * totals[f]
            rows.append(jnp.sum(product, axis=0, keepdims=True))
    seen = jnp.sum(jnp.concatenate(rows, axis=0), axis=1, keepdims=True)
    return jnp.broadcast_to(seen, (2 * OBS, COLS))


def strips(odd, planes, out_a, out_b, at):
    lane = lanes(ROWS)
    left = jnp.zeros((ROWS, COLS), jnp.float32)
    right = left
    for place, plane in enumerate(planes):
        start = SLOT * place
        left = jnp.where((lane >= start) & (lane < start + HALO), plane, left)
        right = jnp.where((lane >= start + HALO) & (lane < start + SLOT), plane, right)
    out_a[at : at + ROWS] = jnp.where(odd, left, right)
    out_b[at : at + ROWS] = jnp.where(odd, right, left)


def first_kernel(
    odd_ref, diffusivity_any, mask_any, weights_any, innovation_any, precision_any, count_any,
    base, send_a, send_b, start_vector, keep,
    diffusivity, mask, weights, innovation, precision, count, sems,
):
    pairs = (
        (innovation_any, innovation), (precision_any, precision), (count_any, count),
        (weights_any, weights), (mask_any, mask), (diffusivity_any, diffusivity),
    )
    copies = [
        pltpu.make_async_copy(source, target, sems.at[place])
        for place, (source, target) in enumerate(pairs)
    ]
    for copy in copies:
        copy.start()
    odd = odd_ref[0] == 1
    for copy in copies[:3]:
        copy.wait()
    valid = count[0, 0]
    for f in range(2):
        for slot in range(OBS):
            at = f * OBS + slot
            kept = jnp.where(slot < valid, precision[f, 0, 0, slot], 0.0)
            keep[at : at + 1] = jnp.full((1, COLS), kept, jnp.float32)
            start_vector[at : at + 1] = jnp.full(
                (1, COLS), kept * innovation[f, 0, 0, slot], jnp.float32
            )
    vector = rounded(start_vector[...])
    start_vector[...] = vector
    copies[3].wait()
    copies[4].wait()
    ocean = mask[...].astype(jnp.float32)
    for f in range(2):
        base[FIELDS + f] = turn(ocean * spread(weights, vector, f), HALO + SLOT * f)
    copies[5].wait()
    for k in range(FIELDS):
        base[k] = turn(diffusivity[k] * ocean, HALO + SLOT * (k % NCAT))
    for f in range(2):
        strips(odd, [base[f * NCAT + c] for c in range(NCAT)], send_a, send_b, f * ROWS)
    strips(odd, [base[FIELDS], base[FIELDS + 1]], send_a, send_b, 2 * ROWS)


def tile(t):
    return slice(8 * t, 8 * t + 8)


def deal(natural, plane):
    parts = [natural[plane, pl.ds(EDGE - HALO + t, 8, stride=TILES), :] for t in range(TILES)]
    return jnp.concatenate(parts, axis=0)


def gather_rows(natural, plane, target):
    for t in range(TILES):
        natural[plane, pl.ds(EDGE - HALO + t, 8, stride=TILES), :] = target[tile(t)]


def pick(lane, places, options, other):
    for place, option in zip(places, options):
        other = jnp.where(lane == place, option, other)
    return other


def east_of(planes, lane):
    turned = [pltpu.roll(plane, COLS - 1, 1) for plane in planes]
    last = [HALO + SLOT * c - 1 for c in range(NCAT)]
    mains = [jnp.where(lane == last[c], turned[NCAT], turned[c]) for c in range(NCAT)]
    return mains + [pick(lane, last, turned[:NCAT], turned[NCAT])]


def west_of(planes, lane):
    turned = [pltpu.roll(plane, 1, 1) for plane in planes]
    head = [HALO + SLOT * c for c in range(NCAT)]
    mains = [jnp.where(lane == head[c], turned[NCAT], turned[c]) for c in range(NCAT)]
    return mains + [pick(lane, head, turned[:NCAT], turned[NCAT])]


def north_tile(ref, at, t):
    return ref[at, tile(t + 1)] if t + 1 < TILES else pltpu.roll(ref[at, tile(0)], 7, 0)


def south_tile(ref, at, t):
    return ref[at, tile(t - 1)] if t > 0 else pltpu.roll(ref[at, tile(TILES - 1)], 1, 0)


def make_faces(scaled, faces):
    lane = lanes(8)
    for g in range(2):
        places = [g * GROUP + c for c in range(GROUP)]
        for t in range(TILES):
            here = [scaled[at, tile(t)] for at in places]
            east = [
                jnp.where((x > 0.0) & (y > 0.0), 0.5 * (x + y), 0.0)
                for x, y in zip(here, east_of(here, lane))
            ]
            west = west_of(east, lane)
            for at, x, e, w in zip(places, here, east, west):
                y = north_tile(scaled, at, t)
                faces[1, at, tile(t)] = e
                faces[2, at, tile(t)] = w
                faces[3, at, tile(t)] = jnp.where((x > 0.0) & (y > 0.0), 0.5 * (x + y), 0.0)
        for t in range(TILES):
            for at in places:
                south = south_tile(faces.at[3], at, t)
                faces[4, at, tile(t)] = south
                faces[0, at, tile(t)] = (
                    1.0 - faces[1, at, tile(t)] - faces[2, at, tile(t)]
                ) - (faces[3, at, tile(t)] + south)


def step(source, target, faces):
    lane = lanes(8)
    for t in range(TILES):
        for g in range(2):
            places = [g * GROUP + c for c in range(GROUP)]
            here = [source[at, tile(t)] for at in places]
            east = east_of(here, lane)
            west = west_of(here, lane)
            for at, x, e, w in zip(places, here, east, west):
                along = faces[1, at, tile(t)] * e + faces[2, at, tile(t)] * w
                across = faces[3, at, tile(t)] * north_tile(source, at, t) + faces[
                    4, at, tile(t)
                ] * south_tile(source, at, t)
                target[at, tile(t)] = faces[0, at, tile(t)] * x + (along + across)


def diffuse(field, other, faces):
    def two(_, carry):
        step(field, other, faces)
        step(other, field, faces)
        return carry

    lax.fori_loop(0, STEPS // 2, two, 0)


def sweep(natural, scaled, faces, weights, out_x, out_y, field, other):
    lane = lanes(DEEP)
    pack = deal(natural, 2)
    for f in range(2):
        main = deal(natural, f)
        side = jnp.zeros((DEEP, COLS), jnp.float32)
        for c in range(NCAT):
            field[f * GROUP + c] = turn(main, SLOT * (c - f))
            start = SLOT * c
            side = jnp.where(
                (lane >= start) & (lane < start + SLOT), turn(pack, SLOT * (c - f)), side
            )
        field[f * GROUP + NCAT] = side
    diffuse(field, other, faces)
    for f in range(2):
        for c in range(GROUP):
            at = f * GROUP + c
            if c < NCAT:
                out_x[f * NCAT + c] = field[at]
            field[at] = jnp.where(scaled[at] > 0.0, field[at], 0.0)
    diffuse(field, other, faces)
    totals = []
    for f in range(2):
        total = jnp.zeros((DEEP, COLS), jnp.float32)
        for c in range(NCAT):
            at = f * GROUP + c
            wet = jnp.where(scaled[at] > 0.0, field[at], 0.0)
            out_y[f * NCAT + c] = wet
            total = total + turn(wet, -HALO - SLOT * c)
        gather_rows(natural, f, total)
        totals.append(natural[f, EDGE:-EDGE])
    return observe(weights, totals)


def second_kernel(
    odd_ref, base, got_a, got_b, above, below, weights, start_vector, keep,
    out_x, out_y, scaled, faces, spread_out, send_a, send_b, vectors,
    natural, field, other,
):
    odd = odd_ref[0] == 1
    planes = FIELDS + 2
    strip = planes * EDGE
    for k in range(planes):
        f, c = divmod(k, NCAT)
        at = f * GROUP + c
        natural[at, :EDGE] = above[k * EDGE : (k + 1) * EDGE]
        natural[at, EDGE:-EDGE] = base[k]
        natural[at, -EDGE:] = below[k * EDGE : (k + 1) * EDGE]
    for p in range(PACKS):
        at = NCAT + GROUP * p
        first = strip + p * EDGE
        second = first + PACKS * EDGE
        natural[at, :EDGE] = above[first : first + EDGE] + above[second : second + EDGE]
        natural[at, EDGE:-EDGE] = (
            got_a[p * ROWS : (p + 1) * ROWS] + got_b[p * ROWS : (p + 1) * ROWS]
        )
        natural[at, -EDGE:] = below[first : first + EDGE] + below[second : second + EDGE]
    for at in range(ALL):
        scaled[at] = deal(natural, at)
    make_faces(scaled, faces)
    for place, at in enumerate((2 * GROUP, 2 * GROUP + 1, 2 * GROUP + NCAT)):
        natural[place] = natural[at]
    seen = sweep(natural, scaled, faces, weights, out_x, out_y, field, other)
    vector = rounded(keep[...] * seen)
    vectors[0] = seen
    vectors[1] = vector
    wet = turn(base[0], -HALO) > 0.0
    for f in range(2):
        spread_out[f] = turn(
            jnp.where(wet, spread(weights, vector, f), 0.0), HALO + SLOT * f
        )
    strips(odd, [spread_out[0], spread_out[1]], send_a, send_b, 0)


def third_kernel(
    spread_in, got_a, got_b, above, below, weights, start_vector, keep,
    scaled, faces, vectors,
    out_x, out_y, sums,
    natural, field, other,
):
    for f in range(2):
        natural[f, :EDGE] = above[f * EDGE : (f + 1) * EDGE]
        natural[f, EDGE:-EDGE] = spread_in[f]
        natural[f, -EDGE:] = below[f * EDGE : (f + 1) * EDGE]
    first, second = slice(2 * EDGE, 3 * EDGE), slice(3 * EDGE, 4 * EDGE)
    natural[2, :EDGE] = above[first] + above[second]
    natural[2, EDGE:-EDGE] = got_a[...] + got_b[...]
    natural[2, -EDGE:] = below[first] + below[second]
    later = sweep(natural, scaled, faces, weights, out_x, out_y, field, other)
    seen = vectors[0]
    vector = vectors[1]
    start = start_vector[...]
    kept = keep[...]
    terms = [
        start * seen, vector * seen, vector * later,
        seen * kept * seen, seen * kept * later, later * kept * later,
    ]
    lane = lanes(1)
    row = jnp.zeros((1, COLS), jnp.float32)
    for place, term in enumerate(terms):
        row = jnp.where(lane == place, jnp.sum(term, axis=0, keepdims=True), row)
    sums[...] = jnp.broadcast_to(row, sums.shape)


def last_kernel(sums, x_first, y_first, x_second, y_second, control, increment, natural):
    row = jnp.sum(sums[...], axis=0, keepdims=True)
    lane = lanes(1)
    a, b, c, k00, k01, k11 = [
        jnp.sum(jnp.where(lane == place, row, 0.0), axis=1, keepdims=True) for place in range(6)
    ]
    b, c, k00, k01, k11 = [value / a for value in (b, c, k00, k01, k11)]
    alpha = 1.0 / (1.0 + b)
    beta = (c - b * b) * alpha * alpha
    share = 1.0 - alpha + beta
    below = (share * share * (1.0 + k00)) - 2.0 * share * alpha * (b + k01) + alpha * alpha * (c + k11)
    later = beta / below
    first = jnp.broadcast_to(alpha + later * share, (DEEP, COLS))
    second = jnp.broadcast_to(-later * alpha, (DEEP, COLS))
    for k in range(FIELDS):
        for place, (out, one, two) in enumerate(
            ((control, x_first, x_second), (increment, y_first, y_second))
        ):
            at = 2 * k + place
            gather_rows(natural, at, first * one[k] + second * two[k])
            out[k] = turn(natural[at, EDGE:-EDGE], -HALO - SLOT * (k % NCAT))


def call(kernel, name, outs, ins, scratch):
    return pl.pallas_call(
        kernel, out_shape=outs, in_specs=ins, out_specs=[VMEM] * len(outs),
        scratch_shapes=scratch, compiler_params=PARAMS, name=name,
    )


SMEM = pl.BlockSpec(memory_space=pltpu.SMEM)
SWEEP = [pltpu.VMEM((ALL, DEEP, COLS), jnp.float32)] * 2


def first_call():
    return call(
        first_kernel, "first",
        (f32(FIELDS + 2, ROWS, COLS), f32(PACKS * ROWS, COLS), f32(PACKS * ROWS, COLS),
         f32(2 * OBS, COLS), f32(2 * OBS, COLS)),
        [SMEM] + [ANY] * 6,
        [pltpu.VMEM((FIELDS, ROWS, COLS), jnp.float32), pltpu.VMEM((ROWS, COLS), jnp.int32),
         pltpu.VMEM((2 * OBS, ROWS, COLS), jnp.bfloat16), pltpu.SMEM((2, 1, 1, OBS), jnp.float32),
         pltpu.SMEM((2, 1, 1, OBS), jnp.float32), pltpu.SMEM((1, 1), jnp.int32),
         pltpu.SemaphoreType.DMA((6,))],
    )


def second_call():
    return call(
        second_kernel, "second",
        (f32(FIELDS, DEEP, COLS), f32(FIELDS, DEEP, COLS), f32(ALL, DEEP, COLS),
         f32(5, ALL, DEEP, COLS), f32(2, ROWS, COLS), f32(ROWS, COLS), f32(ROWS, COLS),
         f32(2, 2 * OBS, COLS)),
        [SMEM] + [VMEM] * 8,
        [pltpu.VMEM((ALL + GROUP, TALL, COLS), jnp.float32)] + SWEEP,
    )


def third_call(lon_count):
    return call(
        third_kernel, "third",
        (f32(FIELDS, DEEP, COLS), f32(FIELDS, DEEP, COLS), f32(lon_count, COLS)),
        [VMEM] * 11,
        [pltpu.VMEM((3, TALL, COLS), jnp.float32)] + SWEEP,
    )


def last_call():
    return call(
        last_kernel, "last",
        (f32(FIELDS, ROWS, COLS), f32(FIELDS, ROWS, COLS)),
        [VMEM] * 5,
        [pltpu.VMEM((2 * FIELDS, TALL, COLS), jnp.float32)],
    )


def per_device(diffusivity, land_mask, obs_weights, innovation, precision_weights, obs_count):
    lat_count = lax.axis_size("lat")
    lon_count = lax.axis_size("lon")
    odd = (lax.axis_index("lon") % 2).astype(jnp.int32).reshape(1)
    down = [(i, i + 1) for i in range(lat_count - 1)]
    up = [(i + 1, i) for i in range(lat_count - 1)]
    chips = [[i, i + 1] for i in range(0, lon_count, 2)]
    between = [(i, (i + 1 if i % 2 else i - 1) % lon_count) for i in range(lon_count)]
    weights = obs_weights.reshape(2 * OBS, ROWS, COLS)

    base, send_a, send_b, start_vector, keep = first_call()(
        odd, diffusivity, land_mask, weights, innovation, precision_weights, obs_count
    )

    def exchange(planes, send_a, send_b):
        got_a = lax.ppermute(send_a, "lon", between)
        both = lax.all_gather(send_b, "lon", axis_index_groups=chips)
        got_b = jnp.where(odd[0] == 1, both[0], both[1])
        packs = send_a.shape[0] // ROWS

        def edge(at):
            parts = [planes[:, at : at + EDGE].reshape(-1, COLS)]
            for got in (got_a, got_b):
                for pack in range(packs):
                    parts.append(got[pack * ROWS + at : pack * ROWS + at + EDGE])
            return jnp.concatenate(parts, axis=0)

        above = lax.ppermute(edge(ROWS - EDGE), "lat", down)
        below = lax.ppermute(edge(0), "lat", up)
        return got_a, got_b, above, below

    x_first, y_first, scaled, faces, spread_first, send_a, send_b, vectors = second_call()(
        odd, base, *exchange(base, send_a, send_b), weights, start_vector, keep
    )
    x_second, y_second, sums = third_call(lon_count)(
        spread_first, *exchange(spread_first, send_a, send_b), weights, start_vector, keep,
        scaled, faces, vectors,
    )
    sums = lax.all_to_all(sums, "lon", 0, 0, tiled=True)
    sums = jnp.broadcast_to(jnp.sum(sums, axis=0, keepdims=True), (lat_count, COLS))
    sums = lax.all_to_all(sums, "lat", 0, 0, tiled=True)
    return last_call()(sums, x_first, y_first, x_second, y_second)


def solution(mesh):
    return jax.shard_map(
        per_device,
        mesh=mesh,
        in_specs=(
            P(None, "lat", "lon"),
            P("lat", "lon"),
            P(None, None, "lat", "lon"),
            P(None, "lat", "lon", None),
            P(None, "lat", "lon", None),
            P("lat", "lon"),
        ),
        out_specs=(P(None, "lat", "lon"), P(None, "lat", "lon")),
        check_vma=False,
    )
```

```python
import jax
import jax.numpy as jnp
from jax import lax
from jax.experimental import pallas as pl
from jax.experimental.pallas import tpu as pltpu
from jax.sharding import PartitionSpec as P

NCAT = 5
FIELDS = 10
OBS = 8
STEPS = 6
HALO = 12
EDGE = 16
ROWS = 32
COLS = 128
TALL = ROWS + 2 * EDGE
TILES = 7
DEEP = 8 * TILES
GROUP = NCAT + 1
ALL = 2 * GROUP
SLOT = 2 * HALO
PACKS = 3
PLANES = FIELDS + 2

VMEM = pl.BlockSpec(memory_space=pltpu.VMEM)
ANY = pl.BlockSpec(memory_space=pltpu.HBM)
FIRST_LIMIT = 62 << 20
PARAMS = pltpu.CompilerParams(vmem_limit_bytes=40 << 20)


def f32(*shape):
    return jax.ShapeDtypeStruct(shape, jnp.float32)


def lanes(rows):
    return lax.broadcasted_iota(jnp.int32, (rows, COLS), 1)


def rounded(values):
    return values.astype(jnp.bfloat16).astype(jnp.float32)


def turn(plane, amount):
    amount = amount % COLS
    return plane if amount == 0 else pltpu.roll(plane, amount, 1)


def spread(weights, vector, f):
    total = weights[f * OBS].astype(jnp.float32) * vector[f * OBS : f * OBS + 1]
    for slot in range(1, OBS):
        at = f * OBS + slot
        total = total + weights[at].astype(jnp.float32) * vector[at : at + 1]
    return total


def observe(weights, totals):
    rows = []
    for f in range(2):
        for slot in range(OBS):
            product = weights[f * OBS + slot].astype(jnp.float32) * totals[f]
            rows.append(jnp.sum(product, axis=0, keepdims=True))
    seen = jnp.sum(jnp.concatenate(rows, axis=0), axis=1, keepdims=True)
    return jnp.broadcast_to(seen, (2 * OBS, COLS))


def strips(odd, planes, out_a, out_b, at):
    lane = lanes(ROWS)
    left = jnp.zeros((ROWS, COLS), jnp.float32)
    right = left
    for place, plane in enumerate(planes):
        start = SLOT * place
        left = jnp.where((lane >= start) & (lane < start + HALO), plane, left)
        right = jnp.where((lane >= start + HALO) & (lane < start + SLOT), plane, right)
    out_a[at : at + ROWS] = jnp.where(odd, left, right)
    out_b[at : at + ROWS] = jnp.where(odd, right, left)


def first_kernel(
    odd_ref, diffusivity_any, mask_any, weights_any, innovation_any, precision_any, count_any,
    base, send_a, send_b,
    diffusivity, mask, weights, innovation, precision, count, sems,
):
    pairs = (
        (innovation_any, innovation), (precision_any, precision), (count_any, count),
        (weights_any, weights), (mask_any, mask), (diffusivity_any, diffusivity),
    )
    copies = [
        pltpu.make_async_copy(source, target, sems.at[place])
        for place, (source, target) in enumerate(pairs)
    ]
    for copy in copies:
        copy.start()
    odd = odd_ref[0] == 1
    for copy in copies[:3]:
        copy.wait()
    valid = count[0, 0]
    for f in range(2):
        for slot in range(OBS):
            at = f * OBS + slot
            kept = jnp.where(slot < valid, precision[f, 0, 0, slot], 0.0)
            base[PLANES, 2 * OBS + at : 2 * OBS + at + 1] = jnp.full((1, COLS), kept, jnp.float32)
            base[PLANES, at : at + 1] = jnp.full(
                (1, COLS), kept * innovation[f, 0, 0, slot], jnp.float32
            )
    vector = rounded(base[PLANES, : 2 * OBS])
    base[PLANES, : 2 * OBS] = vector
    copies[3].wait()
    copies[4].wait()
    ocean = mask[...].astype(jnp.float32)
    for f in range(2):
        base[FIELDS + f] = turn(ocean * spread(weights, vector, f), HALO + SLOT * f)
    copies[5].wait()
    for k in range(FIELDS):
        base[k] = turn(diffusivity[k] * ocean, HALO + SLOT * (k % NCAT))
    for f in range(2):
        strips(odd, [base[f * NCAT + c] for c in range(NCAT)], send_a, send_b, f * ROWS)
    strips(odd, [base[FIELDS], base[FIELDS + 1]], send_a, send_b, 2 * ROWS)


def tile(t):
    return slice(8 * t, 8 * t + 8)


def deal(natural, plane):
    parts = [natural[plane, pl.ds(EDGE - HALO + t, 8, stride=TILES), :] for t in range(TILES)]
    return jnp.concatenate(parts, axis=0)


def gather_rows(natural, plane, target):
    for t in range(TILES):
        natural[plane, pl.ds(EDGE - HALO + t, 8, stride=TILES), :] = target[tile(t)]


def pick(lane, places, options, other):
    for place, option in zip(places, options):
        other = jnp.where(lane == place, option, other)
    return other


def east_of(planes, lane):
    turned = [pltpu.roll(plane, COLS - 1, 1) for plane in planes]
    last = [HALO + SLOT * c - 1 for c in range(NCAT)]
    mains = [jnp.where(lane == last[c], turned[NCAT], turned[c]) for c in range(NCAT)]
    return mains + [pick(lane, last, turned[:NCAT], turned[NCAT])]


def west_of(planes, lane):
    turned = [pltpu.roll(plane, 1, 1) for plane in planes]
    head = [HALO + SLOT * c for c in range(NCAT)]
    mains = [jnp.where(lane == head[c], turned[NCAT], turned[c]) for c in range(NCAT)]
    return mains + [pick(lane, head, turned[:NCAT], turned[NCAT])]


def north_tile(ref, at, t):
    return ref[at, tile(t + 1)] if t + 1 < TILES else pltpu.roll(ref[at, tile(0)], 7, 0)


def south_tile(ref, at, t):
    return ref[at, tile(t - 1)] if t > 0 else pltpu.roll(ref[at, tile(TILES - 1)], 1, 0)


def make_faces(scaled, faces):
    lane = lanes(8)
    for g in range(2):
        places = [g * GROUP + c for c in range(GROUP)]
        for t in range(TILES):
            here = [scaled[at, tile(t)] for at in places]
            east = [
                jnp.where((x > 0.0) & (y > 0.0), 0.5 * (x + y), 0.0)
                for x, y in zip(here, east_of(here, lane))
            ]
            west = west_of(east, lane)
            for at, x, e, w in zip(places, here, east, west):
                y = north_tile(scaled, at, t)
                faces[1, at, tile(t)] = e
                faces[2, at, tile(t)] = w
                faces[3, at, tile(t)] = jnp.where((x > 0.0) & (y > 0.0), 0.5 * (x + y), 0.0)
        for t in range(TILES):
            for at in places:
                south = south_tile(faces.at[3], at, t)
                faces[4, at, tile(t)] = south
                faces[0, at, tile(t)] = (
                    1.0 - faces[1, at, tile(t)] - faces[2, at, tile(t)]
                ) - (faces[3, at, tile(t)] + south)


def step(source, target, faces):
    lane = lanes(8)
    for t in range(TILES):
        for g in range(2):
            places = [g * GROUP + c for c in range(GROUP)]
            here = [source[at, tile(t)] for at in places]
            east = east_of(here, lane)
            west = west_of(here, lane)
            for at, x, e, w in zip(places, here, east, west):
                along = faces[1, at, tile(t)] * e + faces[2, at, tile(t)] * w
                across = faces[3, at, tile(t)] * north_tile(source, at, t) + faces[
                    4, at, tile(t)
                ] * south_tile(source, at, t)
                target[at, tile(t)] = faces[0, at, tile(t)] * x + (along + across)


def diffuse(field, other, faces):
    def two(_, carry):
        step(field, other, faces)
        step(other, field, faces)
        return carry

    lax.fori_loop(0, STEPS // 2, two, 0)


def sweep(natural, scaled, faces, weights, out_x, out_y, field, other):
    lane = lanes(DEEP)
    pack = deal(natural, 2)
    for f in range(2):
        main = deal(natural, f)
        side = jnp.zeros((DEEP, COLS), jnp.float32)
        for c in range(NCAT):
            field[f * GROUP + c] = turn(main, SLOT * (c - f))
            start = SLOT * c
            side = jnp.where(
                (lane >= start) & (lane < start + SLOT), turn(pack, SLOT * (c - f)), side
            )
        field[f * GROUP + NCAT] = side
    diffuse(field, other, faces)
    for f in range(2):
        for c in range(GROUP):
            at = f * GROUP + c
            if c < NCAT:
                k = f * NCAT + c
                gather_rows(natural, k, field[at])
                out_x[k] = natural[k, EDGE:-EDGE]
            field[at] = jnp.where(scaled[at] > 0.0, field[at], 0.0)
    diffuse(field, other, faces)
    totals = []
    for f in range(2):
        total = jnp.zeros((ROWS, COLS), jnp.float32)
        for c in range(NCAT):
            at, k = f * GROUP + c, f * NCAT + c
            gather_rows(natural, k, jnp.where(scaled[at] > 0.0, field[at], 0.0))
            wet = turn(natural[k, EDGE:-EDGE], -HALO - SLOT * c)
            out_y[k] = wet
            total = total + wet
        totals.append(total)
    return observe(weights, totals)


def extend(natural, at, own, above, below, k):
    natural[at, EDGE - HALO : EDGE] = above[k * HALO : (k + 1) * HALO]
    natural[at, EDGE:-EDGE] = own
    natural[at, EDGE + ROWS : EDGE + ROWS + HALO] = below[k * HALO : (k + 1) * HALO]


def second_kernel(
    odd_ref, base, sides, above, below, weights,
    out_x, out_y, scaled, faces, spread_out, send_a, send_b, vectors,
    natural, field, other,
):
    odd = odd_ref[0] == 1
    for k in range(FIELDS + 2 + PACKS):
        if k < FIELDS + 2:
            f, c = divmod(k, NCAT)
            extend(natural, f * GROUP + c, base[k], above, below, k)
        else:
            p = k - FIELDS - 2
            extend(natural, NCAT + GROUP * p, sides[p], above, below, k)
    for at in range(ALL):
        scaled[at] = deal(natural, at)
    make_faces(scaled, faces)
    for place, at in enumerate((2 * GROUP, 2 * GROUP + 1, 2 * GROUP + NCAT)):
        natural[place] = natural[at]
    seen = sweep(natural, scaled, faces, weights, out_x, out_y, field, other)
    keep = base[PLANES, 2 * OBS :]
    vector = rounded(keep * seen)
    vectors[0] = seen
    vectors[1] = vector
    vectors[2] = base[PLANES, : 2 * OBS]
    vectors[3] = keep
    wet = turn(base[0], -HALO) > 0.0
    for f in range(2):
        spread_out[f] = turn(
            jnp.where(wet, spread(weights, vector, f), 0.0), HALO + SLOT * f
        )
    strips(odd, [spread_out[0], spread_out[1]], send_a, send_b, 0)


def third_kernel(
    spread_in, sides, above, below, weights,
    scaled, faces, vectors,
    out_x, out_y, sums,
    natural, field, other,
):
    for k in range(3):
        extend(natural, k, spread_in[k] if k < 2 else sides[0], above, below, k)
    later = sweep(natural, scaled, faces, weights, out_x, out_y, field, other)
    seen = vectors[0]
    vector = vectors[1]
    start = vectors[2]
    kept = vectors[3]
    terms = [
        start * seen, vector * seen, vector * later,
        seen * kept * seen, seen * kept * later, later * kept * later,
    ]
    lane = lanes(1)
    row = jnp.zeros((1, COLS), jnp.float32)
    for place, term in enumerate(terms):
        row = jnp.where(lane == place, jnp.sum(term, axis=0, keepdims=True), row)
    sums[...] = jnp.broadcast_to(row, sums.shape)


def last_kernel(sums, x_first, y_first, x_second, y_second, control, increment):
    row = jnp.sum(sums[...], axis=0, keepdims=True)
    lane = lanes(1)
    a, b, c, k00, k01, k11 = [
        jnp.sum(jnp.where(lane == place, row, 0.0), axis=1, keepdims=True) for place in range(6)
    ]
    b, c, k00, k01, k11 = [value / a for value in (b, c, k00, k01, k11)]
    alpha = 1.0 / (1.0 + b)
    beta = (c - b * b) * alpha * alpha
    share = 1.0 - alpha + beta
    below = (share * share * (1.0 + k00)) - 2.0 * share * alpha * (b + k01) + alpha * alpha * (c + k11)
    later = beta / below
    first = jnp.broadcast_to(alpha + later * share, (ROWS, COLS))
    second = jnp.broadcast_to(-later * alpha, (ROWS, COLS))
    for k in range(FIELDS):
        both = first * x_first[k] + second * x_second[k]
        control[k] = turn(both, -HALO - SLOT * (k % NCAT))
        increment[k] = first * y_first[k] + second * y_second[k]


def call(kernel, name, outs, ins, scratch, params=PARAMS):
    return pl.pallas_call(
        kernel, out_shape=outs, in_specs=ins, out_specs=[VMEM] * len(outs),
        scratch_shapes=scratch, compiler_params=params, name=name,
    )


SMEM = pl.BlockSpec(memory_space=pltpu.SMEM)
SWEEP = [pltpu.VMEM((ALL, DEEP, COLS), jnp.float32)] * 2


def first_call():
    return call(
        first_kernel, "first",
        (f32(PLANES + 1, ROWS, COLS), f32(PACKS * ROWS, COLS), f32(PACKS * ROWS, COLS)),
        [SMEM] + [ANY] * 6,
        [pltpu.VMEM((FIELDS, ROWS, COLS), jnp.float32), pltpu.VMEM((ROWS, COLS), jnp.int32),
         pltpu.VMEM((2 * OBS, ROWS, COLS), jnp.bfloat16), pltpu.SMEM((2, 1, 1, OBS), jnp.float32),
         pltpu.SMEM((2, 1, 1, OBS), jnp.float32), pltpu.SMEM((1, 1), jnp.int32),
         pltpu.SemaphoreType.DMA((6,))],
        pltpu.CompilerParams(vmem_limit_bytes=FIRST_LIMIT),
    )


def second_call():
    return call(
        second_kernel, "second",
        (f32(FIELDS, ROWS, COLS), f32(FIELDS, ROWS, COLS), f32(ALL, DEEP, COLS),
         f32(5, ALL, DEEP, COLS), f32(2, ROWS, COLS), f32(ROWS, COLS), f32(ROWS, COLS),
         f32(4, 2 * OBS, COLS)),
        [SMEM] + [VMEM] * 5,
        [pltpu.VMEM((ALL + GROUP, TALL, COLS), jnp.float32)] + SWEEP,
    )


def third_call(lon_count):
    return call(
        third_kernel, "third",
        (f32(FIELDS, ROWS, COLS), f32(FIELDS, ROWS, COLS), f32(lon_count, COLS)),
        [VMEM] * 8,
        [pltpu.VMEM((FIELDS, TALL, COLS), jnp.float32)] + SWEEP,
    )


def last_call():
    return call(
        last_kernel, "last",
        (f32(FIELDS, ROWS, COLS), f32(FIELDS, ROWS, COLS)),
        [VMEM] * 5,
        [],
    )


def per_device(diffusivity, land_mask, obs_weights, innovation, precision_weights, obs_count):
    lat_count = lax.axis_size("lat")
    lon_count = lax.axis_size("lon")
    odd = (lax.axis_index("lon") % 2).astype(jnp.int32).reshape(1)
    down = [(i, i + 1) for i in range(lat_count - 1)]
    up = [(i + 1, i) for i in range(lat_count - 1)]
    chips = [[i, i + 1] for i in range(0, lon_count, 2)]
    between = [(i, (i + 1 if i % 2 else i - 1) % lon_count) for i in range(lon_count)]
    weights = obs_weights.reshape(2 * OBS, ROWS, COLS)

    base, send_a, send_b = first_call()(
        odd, diffusivity, land_mask, weights, innovation, precision_weights, obs_count
    )

    def exchange(planes, send_a, send_b):
        got_a = lax.ppermute(send_a, "lon", between)
        both = lax.all_gather(send_b, "lon", axis_index_groups=chips)
        sides = got_a + jnp.where(odd[0] == 1, both[0], both[1])
        sides = sides.reshape(-1, ROWS, COLS)

        def edge(at):
            parts = [part[:, at : at + HALO].reshape(-1, COLS) for part in (planes, sides)]
            return jnp.concatenate(parts, axis=0)

        above = lax.ppermute(edge(ROWS - HALO), "lat", down)
        below = lax.ppermute(edge(0), "lat", up)
        return sides, above, below

    x_first, y_first, scaled, faces, spread_first, send_a, send_b, vectors = second_call()(
        odd, base, *exchange(base[:PLANES], send_a, send_b), weights
    )
    x_second, y_second, sums = third_call(lon_count)(
        spread_first, *exchange(spread_first, send_a, send_b), weights, scaled, faces, vectors
    )
    sums = lax.all_to_all(sums, "lon", 0, 0, tiled=True)
    sums = jnp.broadcast_to(jnp.sum(sums, axis=0, keepdims=True), (lat_count, COLS))
    sums = lax.all_to_all(sums, "lat", 0, 0, tiled=True)
    return last_call()(sums, x_first, y_first, x_second, y_second)


def solution(mesh):
    return jax.shard_map(
        per_device,
        mesh=mesh,
        in_specs=(
            P(None, "lat", "lon"),
            P("lat", "lon"),
            P(None, None, "lat", "lon"),
            P(None, "lat", "lon", None),
            P(None, "lat", "lon", None),
            P("lat", "lon"),
        ),
        out_specs=(P(None, "lat", "lon"), P(None, "lat", "lon")),
        check_vma=False,
    )
```

```python
import jax
import jax.numpy as jnp
from jax import lax
from jax.experimental import pallas as pl
from jax.experimental.pallas import tpu as pltpu
from jax.sharding import PartitionSpec as P

NCAT = 5
FIELDS = 10
OBS = 8
STEPS = 6
HALO = 12
EDGE = 16
ROWS = 32
COLS = 128
TALL = ROWS + 2 * EDGE
TILES = 7
DEEP = 8 * TILES
GROUP = NCAT + 1
ALL = 2 * GROUP
SLOT = 2 * HALO
PACKS = 3
PLANES = FIELDS + 2

VMEM = pl.BlockSpec(memory_space=pltpu.VMEM)
ANY = pl.BlockSpec(memory_space=pltpu.HBM)
FIRST_LIMIT = 62 << 20
PARAMS = pltpu.CompilerParams(vmem_limit_bytes=40 << 20)


def f32(*shape):
    return jax.ShapeDtypeStruct(shape, jnp.float32)


def lanes(rows):
    return lax.broadcasted_iota(jnp.int32, (rows, COLS), 1)


def rounded(values):
    return values.astype(jnp.bfloat16).astype(jnp.float32)


def turn(plane, amount):
    amount = amount % COLS
    return plane if amount == 0 else pltpu.roll(plane, amount, 1)


def spread(weights, vector, f):
    total = weights[f * OBS].astype(jnp.float32) * vector[f * OBS : f * OBS + 1]
    for slot in range(1, OBS):
        at = f * OBS + slot
        total = total + weights[at].astype(jnp.float32) * vector[at : at + 1]
    return total


def observe(weights, totals):
    rows = []
    for f in range(2):
        for slot in range(OBS):
            product = weights[f * OBS + slot].astype(jnp.float32) * totals[f]
            rows.append(jnp.sum(product, axis=0, keepdims=True))
    seen = jnp.sum(jnp.concatenate(rows, axis=0), axis=1, keepdims=True)
    return jnp.broadcast_to(seen, (2 * OBS, COLS))


def strips(odd, planes, out_a, out_b, at):
    lane = lanes(ROWS)
    left = jnp.zeros((ROWS, COLS), jnp.float32)
    right = left
    for place, plane in enumerate(planes):
        start = SLOT * place
        left = jnp.where((lane >= start) & (lane < start + HALO), plane, left)
        right = jnp.where((lane >= start + HALO) & (lane < start + SLOT), plane, right)
    out_a[at : at + ROWS] = jnp.where(odd, left, right)
    out_b[at : at + ROWS] = jnp.where(odd, right, left)


def first_kernel(
    odd_ref, diffusivity_any, mask_any, weights_any, innovation_any, precision_any, count_any,
    base, send_a, send_b,
    diffusivity, mask, weights, innovation, precision, count, sems,
):
    pairs = (
        (innovation_any, innovation), (precision_any, precision), (count_any, count),
        (weights_any, weights), (mask_any, mask), (diffusivity_any, diffusivity),
    )
    copies = [
        pltpu.make_async_copy(source, target, sems.at[place])
        for place, (source, target) in enumerate(pairs)
    ]
    for copy in copies:
        copy.start()
    odd = odd_ref[0] == 1
    for copy in copies[:3]:
        copy.wait()
    valid = count[0, 0]
    for f in range(2):
        for slot in range(OBS):
            at = f * OBS + slot
            kept = jnp.where(slot < valid, precision[f, 0, 0, slot], 0.0)
            base[PLANES, 2 * OBS + at : 2 * OBS + at + 1] = jnp.full((1, COLS), kept, jnp.float32)
            base[PLANES, at : at + 1] = jnp.full(
                (1, COLS), kept * innovation[f, 0, 0, slot], jnp.float32
            )
    vector = rounded(base[PLANES, : 2 * OBS])
    base[PLANES, : 2 * OBS] = vector
    copies[3].wait()
    copies[4].wait()
    ocean = mask[...].astype(jnp.float32)
    for f in range(2):
        base[FIELDS + f] = turn(ocean * spread(weights, vector, f), HALO + SLOT * f)
    copies[5].wait()
    for k in range(FIELDS):
        base[k] = turn(diffusivity[k] * ocean, HALO + SLOT * (k % NCAT))
    for f in range(2):
        strips(odd, [base[f * NCAT + c] for c in range(NCAT)], send_a, send_b, f * ROWS)
    strips(odd, [base[FIELDS], base[FIELDS + 1]], send_a, send_b, 2 * ROWS)


def tile(t):
    return slice(8 * t, 8 * t + 8)


def deal(natural, plane):
    parts = [natural[plane, pl.ds(EDGE - HALO + t, 8, stride=TILES), :] for t in range(TILES)]
    return jnp.concatenate(parts, axis=0)


def gather_rows(natural, plane, target):
    for t in range(TILES):
        natural[plane, pl.ds(EDGE - HALO + t, 8, stride=TILES), :] = target[tile(t)]


def pick(lane, places, options, other):
    for place, option in zip(places, options):
        other = jnp.where(lane == place, option, other)
    return other


def east_of(planes, lane):
    turned = [pltpu.roll(plane, COLS - 1, 1) for plane in planes]
    last = [HALO + SLOT * c - 1 for c in range(NCAT)]
    mains = [jnp.where(lane == last[c], turned[NCAT], turned[c]) for c in range(NCAT)]
    return mains + [pick(lane, last, turned[:NCAT], turned[NCAT])]


def west_of(planes, lane):
    turned = [pltpu.roll(plane, 1, 1) for plane in planes]
    head = [HALO + SLOT * c for c in range(NCAT)]
    mains = [jnp.where(lane == head[c], turned[NCAT], turned[c]) for c in range(NCAT)]
    return mains + [pick(lane, head, turned[:NCAT], turned[NCAT])]


def north_tile(ref, at, t):
    return ref[at, tile(t + 1)] if t + 1 < TILES else pltpu.roll(ref[at, tile(0)], 7, 0)


def make_faces(scaled, faces):
    lane = lanes(8)
    for g in range(2):
        places = [g * GROUP + c for c in range(GROUP)]
        for t in range(TILES):
            here = [scaled[at, tile(t)] for at in places]
            east = [
                jnp.where((x > 0.0) & (y > 0.0), 0.5 * (x + y), 0.0)
                for x, y in zip(here, east_of(here, lane))
            ]
            west = west_of(east, lane)
            for at, x, e, w in zip(places, here, east, west):
                y = north_tile(scaled, at, t)
                faces[0, at, tile(t)] = e
                faces[1, at, tile(t)] = w
                faces[2, at, tile(t)] = jnp.where((x > 0.0) & (y > 0.0), 0.5 * (x + y), 0.0)


def step(source, target, faces):
    lane = lanes(8)
    for g in range(2):
        places = [g * GROUP + c for c in range(GROUP)]
        north = {}
        for at in places:
            for t in range(TILES):
                north[at, t] = faces[2, at, tile(t)] * (
                    north_tile(source, at, t) - source[at, tile(t)]
                )
        for t in range(TILES):
            here = [source[at, tile(t)] for at in places]
            east = east_of(here, lane)
            west = west_of(here, lane)
            for at, x, e, w in zip(places, here, east, west):
                along = faces[0, at, tile(t)] * (e - x) + faces[1, at, tile(t)] * (w - x)
                south = north[at, t - 1] if t > 0 else pltpu.roll(north[at, TILES - 1], 1, 0)
                target[at, tile(t)] = x + (along + (north[at, t] - south))


def diffuse(field, other, faces):
    for _ in range(STEPS // 2):
        step(field, other, faces)
        step(other, field, faces)


def sweep(natural, scaled, faces, weights, out_x, out_y, field, other):
    lane = lanes(DEEP)
    pack = deal(natural, 2)
    for f in range(2):
        main = deal(natural, f)
        side = jnp.zeros((DEEP, COLS), jnp.float32)
        for c in range(NCAT):
            field[f * GROUP + c] = turn(main, SLOT * (c - f))
            start = SLOT * c
            side = jnp.where(
                (lane >= start) & (lane < start + SLOT), turn(pack, SLOT * (c - f)), side
            )
        field[f * GROUP + NCAT] = side
    diffuse(field, other, faces)
    for f in range(2):
        for c in range(GROUP):
            at = f * GROUP + c
            if c < NCAT:
                k = f * NCAT + c
                gather_rows(natural, k, field[at])
                out_x[k] = natural[k, EDGE:-EDGE]
            field[at] = jnp.where(scaled[at] > 0.0, field[at], 0.0)
    diffuse(field, other, faces)
    totals = []
    for f in range(2):
        total = jnp.zeros((ROWS, COLS), jnp.float32)
        for c in range(NCAT):
            at, k = f * GROUP + c, f * NCAT + c
            gather_rows(natural, k, jnp.where(scaled[at] > 0.0, field[at], 0.0))
            wet = turn(natural[k, EDGE:-EDGE], -HALO - SLOT * c)
            out_y[k] = wet
            total = total + wet
        totals.append(total)
    return observe(weights, totals)


def extend(natural, at, own, above, below, k):
    natural[at, EDGE - HALO : EDGE] = above[k * HALO : (k + 1) * HALO]
    natural[at, EDGE:-EDGE] = own
    natural[at, EDGE + ROWS : EDGE + ROWS + HALO] = below[k * HALO : (k + 1) * HALO]


def second_kernel(
    odd_ref, base, sides, above, below, weights,
    out_x, out_y, scaled, faces, spread_out, send_a, send_b, vectors,
    natural, field, other,
):
    odd = odd_ref[0] == 1
    for k in range(FIELDS + 2 + PACKS):
        if k < FIELDS + 2:
            f, c = divmod(k, NCAT)
            extend(natural, f * GROUP + c, base[k], above, below, k)
        else:
            p = k - FIELDS - 2
            extend(natural, NCAT + GROUP * p, sides[p], above, below, k)
    for at in range(ALL):
        scaled[at] = deal(natural, at)
    make_faces(scaled, faces)
    for place, at in enumerate((2 * GROUP, 2 * GROUP + 1, 2 * GROUP + NCAT)):
        natural[place] = natural[at]
    seen = sweep(natural, scaled, faces, weights, out_x, out_y, field, other)
    keep = base[PLANES, 2 * OBS :]
    vector = rounded(keep * seen)
    vectors[0] = seen
    vectors[1] = vector
    vectors[2] = base[PLANES, : 2 * OBS]
    vectors[3] = keep
    wet = turn(base[0], -HALO) > 0.0
    for f in range(2):
        spread_out[f] = turn(
            jnp.where(wet, spread(weights, vector, f), 0.0), HALO + SLOT * f
        )
    strips(odd, [spread_out[0], spread_out[1]], send_a, send_b, 0)


def third_kernel(
    spread_in, sides, above, below, weights,
    scaled, faces, vectors,
    out_x, out_y, sums,
    natural, field, other,
):
    for k in range(3):
        extend(natural, k, spread_in[k] if k < 2 else sides[0], above, below, k)
    later = sweep(natural, scaled, faces, weights, out_x, out_y, field, other)
    seen = vectors[0]
    vector = vectors[1]
    start = vectors[2]
    kept = vectors[3]
    terms = [
        start * seen, vector * seen, vector * later,
        seen * kept * seen, seen * kept * later, later * kept * later,
    ]
    lane = lanes(1)
    row = jnp.zeros((1, COLS), jnp.float32)
    for place, term in enumerate(terms):
        row = jnp.where(lane == place, jnp.sum(term, axis=0, keepdims=True), row)
    sums[...] = jnp.broadcast_to(row, sums.shape)


def last_kernel(sums, x_first, y_first, x_second, y_second, control, increment):
    row = jnp.sum(sums[...], axis=0, keepdims=True)
    lane = lanes(1)
    a, b, c, k00, k01, k11 = [
        jnp.sum(jnp.where(lane == place, row, 0.0), axis=1, keepdims=True) for place in range(6)
    ]
    b, c, k00, k01, k11 = [value / a for value in (b, c, k00, k01, k11)]
    alpha = 1.0 / (1.0 + b)
    beta = (c - b * b) * alpha * alpha
    share = 1.0 - alpha + beta
    below = (share * share * (1.0 + k00)) - 2.0 * share * alpha * (b + k01) + alpha * alpha * (c + k11)
    later = beta / below
    first = jnp.broadcast_to(alpha + later * share, (ROWS, COLS))
    second = jnp.broadcast_to(-later * alpha, (ROWS, COLS))
    for k in range(FIELDS):
        both = first * x_first[k] + second * x_second[k]
        control[k] = turn(both, -HALO - SLOT * (k % NCAT))
        increment[k] = first * y_first[k] + second * y_second[k]


def call(kernel, name, outs, ins, scratch, params=PARAMS):
    return pl.pallas_call(
        kernel, out_shape=outs, in_specs=ins, out_specs=[VMEM] * len(outs),
        scratch_shapes=scratch, compiler_params=params, name=name,
    )


SMEM = pl.BlockSpec(memory_space=pltpu.SMEM)
SWEEP = [pltpu.VMEM((ALL, DEEP, COLS), jnp.float32)] * 2


def first_call():
    return call(
        first_kernel, "first",
        (f32(PLANES + 1, ROWS, COLS), f32(PACKS * ROWS, COLS), f32(PACKS * ROWS, COLS)),
        [SMEM] + [ANY] * 6,
        [pltpu.VMEM((FIELDS, ROWS, COLS), jnp.float32), pltpu.VMEM((ROWS, COLS), jnp.int32),
         pltpu.VMEM((2 * OBS, ROWS, COLS), jnp.bfloat16), pltpu.SMEM((2, 1, 1, OBS), jnp.float32),
         pltpu.SMEM((2, 1, 1, OBS), jnp.float32), pltpu.SMEM((1, 1), jnp.int32),
         pltpu.SemaphoreType.DMA((6,))],
        pltpu.CompilerParams(vmem_limit_bytes=FIRST_LIMIT),
    )


def second_call():
    return call(
        second_kernel, "second",
        (f32(FIELDS, ROWS, COLS), f32(FIELDS, ROWS, COLS), f32(ALL, DEEP, COLS),
         f32(3, ALL, DEEP, COLS), f32(2, ROWS, COLS), f32(ROWS, COLS), f32(ROWS, COLS),
         f32(4, 2 * OBS, COLS)),
        [SMEM] + [VMEM] * 5,
        [pltpu.VMEM((ALL + GROUP, TALL, COLS), jnp.float32)] + SWEEP,
    )


def third_call(lon_count):
    return call(
        third_kernel, "third",
        (f32(FIELDS, ROWS, COLS), f32(FIELDS, ROWS, COLS), f32(lon_count, COLS)),
        [VMEM] * 8,
        [pltpu.VMEM((FIELDS, TALL, COLS), jnp.float32)] + SWEEP,
    )


def last_call():
    return call(
        last_kernel, "last",
        (f32(FIELDS, ROWS, COLS), f32(FIELDS, ROWS, COLS)),
        [VMEM] * 5,
        [],
    )


def per_device(diffusivity, land_mask, obs_weights, innovation, precision_weights, obs_count):
    lat_count = lax.axis_size("lat")
    lon_count = lax.axis_size("lon")
    odd = (lax.axis_index("lon") % 2).astype(jnp.int32).reshape(1)
    down = [(i, i + 1) for i in range(lat_count - 1)]
    up = [(i + 1, i) for i in range(lat_count - 1)]
    chips = [[i, i + 1] for i in range(0, lon_count, 2)]
    between = [(i, (i + 1 if i % 2 else i - 1) % lon_count) for i in range(lon_count)]
    weights = obs_weights.reshape(2 * OBS, ROWS, COLS)

    base, send_a, send_b = first_call()(
        odd, diffusivity, land_mask, weights, innovation, precision_weights, obs_count
    )

    def exchange(planes, send_a, send_b):
        got_a = lax.ppermute(send_a, "lon", between)
        both = lax.all_gather(send_b, "lon", axis_index_groups=chips)
        planes, both = lax.optimization_barrier((planes, both))
        sides = got_a + jnp.where(odd[0] == 1, both[0], both[1])
        sides = sides.reshape(-1, ROWS, COLS)

        def edge(at):
            parts = [part[:, at : at + HALO].reshape(-1, COLS) for part in (planes[:PLANES], sides)]
            return jnp.concatenate(parts, axis=0)

        above = lax.ppermute(edge(ROWS - HALO), "lat", down)
        below = lax.ppermute(edge(0), "lat", up)
        return sides, above, below

    x_first, y_first, scaled, faces, spread_first, send_a, send_b, vectors = second_call()(
        odd, base, *exchange(base, send_a, send_b), weights
    )
    x_second, y_second, sums = third_call(lon_count)(
        spread_first, *exchange(spread_first, send_a, send_b), weights, scaled, faces, vectors
    )
    sums = lax.all_to_all(sums, "lon", 0, 0, tiled=True)
    sums = jnp.broadcast_to(jnp.sum(sums, axis=0, keepdims=True), (lat_count, COLS))
    sums = lax.all_to_all(sums, "lat", 0, 0, tiled=True)
    return last_call()(sums, x_first, y_first, x_second, y_second)


def solution(mesh):
    return jax.shard_map(
        per_device,
        mesh=mesh,
        in_specs=(
            P(None, "lat", "lon"),
            P("lat", "lon"),
            P(None, None, "lat", "lon"),
            P(None, "lat", "lon", None),
            P(None, "lat", "lon", None),
            P("lat", "lon"),
        ),
        out_specs=(P(None, "lat", "lon"), P(None, "lat", "lon")),
        check_vma=False,
    )
```

```python
import jax
import jax.numpy as jnp
from jax import lax
from jax.experimental import pallas as pl
from jax.experimental.pallas import tpu as pltpu
from jax.sharding import PartitionSpec as P

NCAT = 5
FIELDS = 10
OBS = 8
STEPS = 6
HALO = 12
EDGE = 16
ROWS = 32
COLS = 128
TALL = ROWS + 2 * EDGE
TILES = 7
DEEP = 8 * TILES
GROUP = NCAT + 1
ALL = 2 * GROUP
SLOT = 2 * HALO
PACKS = 3
PLANES = FIELDS + 2

VMEM = pl.BlockSpec(memory_space=pltpu.VMEM)
ANY = pl.BlockSpec(memory_space=pltpu.HBM)
FIRST_LIMIT = 62 << 20
PARAMS = pltpu.CompilerParams(vmem_limit_bytes=40 << 20)


def f32(*shape):
    return jax.ShapeDtypeStruct(shape, jnp.float32)


def lanes(rows):
    return lax.broadcasted_iota(jnp.int32, (rows, COLS), 1)


def rounded(values):
    return values.astype(jnp.bfloat16).astype(jnp.float32)


def turn(plane, amount):
    amount = amount % COLS
    return plane if amount == 0 else pltpu.roll(plane, amount, 1)


def spread(weights, vector, f):
    total = weights[f * OBS].astype(jnp.float32) * vector[f * OBS : f * OBS + 1]
    for slot in range(1, OBS):
        at = f * OBS + slot
        total = total + weights[at].astype(jnp.float32) * vector[at : at + 1]
    return total


def observe(weights, totals):
    rows = []
    for f in range(2):
        for slot in range(OBS):
            product = weights[f * OBS + slot].astype(jnp.float32) * totals[f]
            rows.append(jnp.sum(product, axis=0, keepdims=True))
    seen = jnp.sum(jnp.concatenate(rows, axis=0), axis=1, keepdims=True)
    return jnp.broadcast_to(seen, (2 * OBS, COLS))


def strips(odd, planes, out_a, out_b, at):
    lane = lanes(ROWS)
    left = jnp.zeros((ROWS, COLS), jnp.float32)
    right = left
    for place, plane in enumerate(planes):
        start = SLOT * place
        left = jnp.where((lane >= start) & (lane < start + HALO), plane, left)
        right = jnp.where((lane >= start + HALO) & (lane < start + SLOT), plane, right)
    out_a[at : at + ROWS] = jnp.where(odd, left, right)
    out_b[at : at + ROWS] = jnp.where(odd, right, left)


def first_kernel(
    odd_ref, diffusivity_any, mask_any, weights_any, innovation_any, precision_any, count_any,
    base, send_a, send_b, edges,
    diffusivity, mask, weights, innovation, precision, count, sems,
):
    pairs = (
        (innovation_any, innovation), (precision_any, precision), (count_any, count),
        (weights_any, weights), (mask_any, mask), (diffusivity_any, diffusivity),
    )
    copies = [
        pltpu.make_async_copy(source, target, sems.at[place])
        for place, (source, target) in enumerate(pairs)
    ]
    for copy in copies:
        copy.start()
    odd = odd_ref[0] == 1
    for copy in copies[:3]:
        copy.wait()
    valid = count[0, 0]
    for f in range(2):
        for slot in range(OBS):
            at = f * OBS + slot
            kept = jnp.where(slot < valid, precision[f, 0, 0, slot], 0.0)
            base[PLANES, 2 * OBS + at : 2 * OBS + at + 1] = jnp.full((1, COLS), kept, jnp.float32)
            base[PLANES, at : at + 1] = jnp.full(
                (1, COLS), kept * innovation[f, 0, 0, slot], jnp.float32
            )
    vector = rounded(base[PLANES, : 2 * OBS])
    base[PLANES, : 2 * OBS] = vector
    copies[3].wait()
    copies[4].wait()
    ocean = mask[...].astype(jnp.float32)
    for f in range(2):
        base[FIELDS + f] = turn(ocean * spread(weights, vector, f), HALO + SLOT * f)
    copies[5].wait()
    for k in range(FIELDS):
        base[k] = turn(diffusivity[k] * ocean, HALO + SLOT * (k % NCAT))
    for f in range(2):
        strips(odd, [base[f * NCAT + c] for c in range(NCAT)], send_a, send_b, f * ROWS)
    strips(odd, [base[FIELDS], base[FIELDS + 1]], send_a, send_b, 2 * ROWS)
    for k in range(PLANES):
        edges[0, HALO * k : HALO * (k + 1)] = base[k, :HALO]
        edges[1, HALO * k : HALO * (k + 1)] = base[k, ROWS - HALO :]


def tile(t):
    return slice(8 * t, 8 * t + 8)


def deal(natural, plane):
    parts = [natural[plane, pl.ds(EDGE - HALO + t, 8, stride=TILES), :] for t in range(TILES)]
    return jnp.concatenate(parts, axis=0)


def gather_rows(natural, plane, target):
    for t in range(TILES):
        natural[plane, pl.ds(EDGE - HALO + t, 8, stride=TILES), :] = target[tile(t)]


def pick(lane, places, options, other):
    for place, option in zip(places, options):
        other = jnp.where(lane == place, option, other)
    return other


def east_of(planes, lane):
    turned = [pltpu.roll(plane, COLS - 1, 1) for plane in planes]
    last = [HALO + SLOT * c - 1 for c in range(NCAT)]
    mains = [jnp.where(lane == last[c], turned[NCAT], turned[c]) for c in range(NCAT)]
    return mains + [pick(lane, last, turned[:NCAT], turned[NCAT])]


def west_of(planes, lane):
    turned = [pltpu.roll(plane, 1, 1) for plane in planes]
    head = [HALO + SLOT * c for c in range(NCAT)]
    mains = [jnp.where(lane == head[c], turned[NCAT], turned[c]) for c in range(NCAT)]
    return mains + [pick(lane, head, turned[:NCAT], turned[NCAT])]


def north_tile(ref, at, t):
    return ref[at, tile(t + 1)] if t + 1 < TILES else pltpu.roll(ref[at, tile(0)], 7, 0)


def make_faces(scaled, faces):
    lane = lanes(8)
    for g in range(2):
        places = [g * GROUP + c for c in range(GROUP)]
        for t in range(TILES):
            here = [scaled[at, tile(t)] for at in places]
            east = [
                jnp.where((x > 0.0) & (y > 0.0), 0.5 * (x + y), 0.0)
                for x, y in zip(here, east_of(here, lane))
            ]
            west = west_of(east, lane)
            for at, x, e, w in zip(places, here, east, west):
                y = north_tile(scaled, at, t)
                faces[0, at, tile(t)] = e
                faces[1, at, tile(t)] = w
                faces[2, at, tile(t)] = jnp.where((x > 0.0) & (y > 0.0), 0.5 * (x + y), 0.0)


def step(source, target, faces):
    lane = lanes(8)
    for g in range(2):
        places = [g * GROUP + c for c in range(GROUP)]
        north = {}
        for at in places:
            for t in range(TILES):
                north[at, t] = faces[2, at, tile(t)] * (
                    north_tile(source, at, t) - source[at, tile(t)]
                )
        for t in range(TILES):
            here = [source[at, tile(t)] for at in places]
            east = east_of(here, lane)
            west = west_of(here, lane)
            for at, x, e, w in zip(places, here, east, west):
                along = faces[0, at, tile(t)] * (e - x) + faces[1, at, tile(t)] * (w - x)
                south = north[at, t - 1] if t > 0 else pltpu.roll(north[at, TILES - 1], 1, 0)
                target[at, tile(t)] = x + (along + (north[at, t] - south))


def diffuse(field, other, faces):
    for _ in range(STEPS // 2):
        step(field, other, faces)
        step(other, field, faces)


def sweep(natural, scaled, faces, weights, out_x, out_y, field, other):
    lane = lanes(DEEP)
    pack = deal(natural, 2)
    for f in range(2):
        main = deal(natural, f)
        side = jnp.zeros((DEEP, COLS), jnp.float32)
        for c in range(NCAT):
            field[f * GROUP + c] = turn(main, SLOT * (c - f))
            start = SLOT * c
            side = jnp.where(
                (lane >= start) & (lane < start + SLOT), turn(pack, SLOT * (c - f)), side
            )
        field[f * GROUP + NCAT] = side
    diffuse(field, other, faces)
    for f in range(2):
        for c in range(GROUP):
            at = f * GROUP + c
            if c < NCAT:
                k = f * NCAT + c
                gather_rows(natural, k, field[at])
                out_x[k] = natural[k, EDGE:-EDGE]
            field[at] = jnp.where(scaled[at] > 0.0, field[at], 0.0)
    diffuse(field, other, faces)
    totals = []
    for f in range(2):
        total = jnp.zeros((ROWS, COLS), jnp.float32)
        for c in range(NCAT):
            at, k = f * GROUP + c, f * NCAT + c
            gather_rows(natural, k, jnp.where(scaled[at] > 0.0, field[at], 0.0))
            wet = turn(natural[k, EDGE:-EDGE], -HALO - SLOT * c)
            out_y[k] = wet
            total = total + wet
        totals.append(total)
    return observe(weights, totals)


def extend(natural, at, own, above, below, k):
    natural[at, EDGE - HALO : EDGE] = above[k * HALO : (k + 1) * HALO]
    natural[at, EDGE:-EDGE] = own
    natural[at, EDGE + ROWS : EDGE + ROWS + HALO] = below[k * HALO : (k + 1) * HALO]


def second_kernel(
    odd_ref, base, sides, above, below, weights,
    out_x, out_y, scaled, faces, spread_out, send_a, send_b, vectors, edges,
    natural, field, other,
):
    odd = odd_ref[0] == 1
    for k in range(FIELDS + 2 + PACKS):
        if k < FIELDS + 2:
            f, c = divmod(k, NCAT)
            extend(natural, f * GROUP + c, base[k], above, below, k)
        else:
            p = k - FIELDS - 2
            extend(natural, NCAT + GROUP * p, sides[p], above, below, k)
    for at in range(ALL):
        scaled[at] = deal(natural, at)
    make_faces(scaled, faces)
    for place, at in enumerate((2 * GROUP, 2 * GROUP + 1, 2 * GROUP + NCAT)):
        natural[place] = natural[at]
    seen = sweep(natural, scaled, faces, weights, out_x, out_y, field, other)
    keep = base[PLANES, 2 * OBS :]
    vector = rounded(keep * seen)
    vectors[0] = seen
    vectors[1] = vector
    vectors[2] = base[PLANES, : 2 * OBS]
    vectors[3] = keep
    wet = turn(base[0], -HALO) > 0.0
    for f in range(2):
        spread_out[f] = turn(
            jnp.where(wet, spread(weights, vector, f), 0.0), HALO + SLOT * f
        )
    strips(odd, [spread_out[0], spread_out[1]], send_a, send_b, 0)
    for f in range(2):
        edges[0, HALO * f : HALO * (f + 1)] = spread_out[f, :HALO]
        edges[1, HALO * f : HALO * (f + 1)] = spread_out[f, ROWS - HALO :]


def third_kernel(
    spread_in, sides, above, below, weights,
    scaled, faces, vectors,
    out_x, out_y, sums,
    natural, field, other,
):
    for k in range(3):
        extend(natural, k, spread_in[k] if k < 2 else sides[0], above, below, k)
    later = sweep(natural, scaled, faces, weights, out_x, out_y, field, other)
    seen = vectors[0]
    vector = vectors[1]
    start = vectors[2]
    kept = vectors[3]
    terms = [
        start * seen, vector * seen, vector * later,
        seen * kept * seen, seen * kept * later, later * kept * later,
    ]
    lane = lanes(1)
    row = jnp.zeros((1, COLS), jnp.float32)
    for place, term in enumerate(terms):
        row = jnp.where(lane == place, jnp.sum(term, axis=0, keepdims=True), row)
    sums[...] = jnp.broadcast_to(row, sums.shape)


def last_kernel(sums, x_first, y_first, x_second, y_second, control, increment):
    row = jnp.sum(sums[...], axis=0, keepdims=True)
    lane = lanes(1)
    a, b, c, k00, k01, k11 = [
        jnp.sum(jnp.where(lane == place, row, 0.0), axis=1, keepdims=True) for place in range(6)
    ]
    b, c, k00, k01, k11 = [value / a for value in (b, c, k00, k01, k11)]
    alpha = 1.0 / (1.0 + b)
    beta = (c - b * b) * alpha * alpha
    share = 1.0 - alpha + beta
    below = (share * share * (1.0 + k00)) - 2.0 * share * alpha * (b + k01) + alpha * alpha * (c + k11)
    later = beta / below
    first = jnp.broadcast_to(alpha + later * share, (ROWS, COLS))
    second = jnp.broadcast_to(-later * alpha, (ROWS, COLS))
    for k in range(FIELDS):
        both = first * x_first[k] + second * x_second[k]
        control[k] = turn(both, -HALO - SLOT * (k % NCAT))
        increment[k] = first * y_first[k] + second * y_second[k]


def call(kernel, name, outs, ins, scratch, params=PARAMS):
    return pl.pallas_call(
        kernel, out_shape=outs, in_specs=ins, out_specs=[VMEM] * len(outs),
        scratch_shapes=scratch, compiler_params=params, name=name,
    )


SMEM = pl.BlockSpec(memory_space=pltpu.SMEM)
SWEEP = [pltpu.VMEM((ALL, DEEP, COLS), jnp.float32)] * 2


def first_call():
    return call(
        first_kernel, "first",
        (f32(PLANES + 1, ROWS, COLS), f32(PACKS * ROWS, COLS), f32(PACKS * ROWS, COLS),
         f32(2, HALO * PLANES, COLS)),
        [SMEM] + [ANY] * 6,
        [pltpu.VMEM((FIELDS, ROWS, COLS), jnp.float32), pltpu.VMEM((ROWS, COLS), jnp.int32),
         pltpu.VMEM((2 * OBS, ROWS, COLS), jnp.bfloat16), pltpu.SMEM((2, 1, 1, OBS), jnp.float32),
         pltpu.SMEM((2, 1, 1, OBS), jnp.float32), pltpu.SMEM((1, 1), jnp.int32),
         pltpu.SemaphoreType.DMA((6,))],
        pltpu.CompilerParams(vmem_limit_bytes=FIRST_LIMIT),
    )


def second_call():
    return call(
        second_kernel, "second",
        (f32(FIELDS, ROWS, COLS), f32(FIELDS, ROWS, COLS), f32(ALL, DEEP, COLS),
         f32(3, ALL, DEEP, COLS), f32(2, ROWS, COLS), f32(ROWS, COLS), f32(ROWS, COLS),
         f32(4, 2 * OBS, COLS), f32(2, 2 * HALO, COLS)),
        [SMEM] + [VMEM] * 5,
        [pltpu.VMEM((ALL + GROUP, TALL, COLS), jnp.float32)] + SWEEP,
    )


def third_call(lon_count):
    return call(
        third_kernel, "third",
        (f32(FIELDS, ROWS, COLS), f32(FIELDS, ROWS, COLS), f32(lon_count, COLS)),
        [VMEM] * 8,
        [pltpu.VMEM((FIELDS, TALL, COLS), jnp.float32)] + SWEEP,
    )


def last_call():
    return call(
        last_kernel, "last",
        (f32(FIELDS, ROWS, COLS), f32(FIELDS, ROWS, COLS)),
        [VMEM] * 5,
        [],
    )


def per_device(diffusivity, land_mask, obs_weights, innovation, precision_weights, obs_count):
    lat_count = lax.axis_size("lat")
    lon_count = lax.axis_size("lon")
    odd = (lax.axis_index("lon") % 2).astype(jnp.int32).reshape(1)
    down = [(i, i + 1) for i in range(lat_count - 1)]
    up = [(i + 1, i) for i in range(lat_count - 1)]
    chips = [[i, i + 1] for i in range(0, lon_count, 2)]
    between = [(i, (i + 1 if i % 2 else i - 1) % lon_count) for i in range(lon_count)]
    weights = obs_weights.reshape(2 * OBS, ROWS, COLS)

    base, send_a, send_b, edges = first_call()(
        odd, diffusivity, land_mask, weights, innovation, precision_weights, obs_count
    )

    def exchange(edges, send_a, send_b):
        got_a = lax.ppermute(send_a, "lon", between)
        both = lax.all_gather(send_b, "lon", axis_index_groups=chips)
        edges, both = lax.optimization_barrier((edges, both))
        sides = got_a + jnp.where(odd[0] == 1, both[0], both[1])
        sides = sides.reshape(-1, ROWS, COLS)

        def edge(which, at):
            return jnp.concatenate(
                [edges[which], sides[:, at : at + HALO].reshape(-1, COLS)], axis=0
            )

        above = lax.ppermute(edge(1, ROWS - HALO), "lat", down)
        below = lax.ppermute(edge(0, 0), "lat", up)
        return sides, above, below

    x_first, y_first, scaled, faces, spread_first, send_a, send_b, vectors, edges = second_call()(
        odd, base, *exchange(edges, send_a, send_b), weights
    )
    x_second, y_second, sums = third_call(lon_count)(
        spread_first, *exchange(edges, send_a, send_b), weights, scaled, faces, vectors
    )
    sums = lax.all_to_all(sums, "lon", 0, 0, tiled=True)
    sums = jnp.broadcast_to(jnp.sum(sums, axis=0, keepdims=True), (lat_count, COLS))
    sums = lax.all_to_all(sums, "lat", 0, 0, tiled=True)
    return last_call()(sums, x_first, y_first, x_second, y_second)


def solution(mesh):
    return jax.shard_map(
        per_device,
        mesh=mesh,
        in_specs=(
            P(None, "lat", "lon"),
            P("lat", "lon"),
            P(None, None, "lat", "lon"),
            P(None, "lat", "lon", None),
            P(None, "lat", "lon", None),
            P("lat", "lon"),
        ),
        out_specs=(P(None, "lat", "lon"), P(None, "lat", "lon")),
        check_vma=False,
    )
```
